32 devices in a mesh: dev: 8 (over z, y), rep: 4 (over x, core).
Axes of the slice: x: 2, y: 2, z: 4, core: 2. Of those that a mesh axis runs over, the one named last changes fastest.
Arguments:
- spins: int32 [8, 64], P('dev'), may hold values 0 or 1
- activations: float32 [4, 8, 64, 128], P('rep', 'dev'), may hold values from 0 to 0.5
- gradients: float32 [4, 8, 64, 256], P('rep', 'dev'), may hold values from -0.1 to 0.3
Outputs:
- gram: float32 [8, 8], P('dev', 'rep')
The draws below stay inside these ranges and needn't reach their ends.
Inputs may be any that keep to these rules, and one draw needn't show every extreme that they name: `spins`: 1 marks an occupied site, 0 an empty one.
All inputs are finite; a program needn't handle non-finite values. No bound on the sum of `spins` on one device may be relied on, other than what follows from the above.
Results may differ from the reference program's by a relative error of at most 0.0001.
Values sent between devices are 32-bit elements; how exact they have to be, the bound alone decides.
No kernel may reach another device: no remote copies, remote signals or barrier semaphores. Data moves between devices by JAX's collectives and lax.ppermute only.
A program may use at most 128 MiB of HBM per device.

```python
import jax
import jax.numpy as jnp
from jax import lax

A = 128
B = 256
PANELS = 4
L = 64
NS = 8


def with_ends(entries, stream_key, low, high):
    spot = [jax.random.randint(jax.random.fold_in(stream_key, axis), (), 0, length) for axis, length in enumerate(entries.shape)]
    longest = entries.shape.index(max(entries.shape))
    next_to = spot[:longest] + [(spot[longest] + 1) % entries.shape[longest]] + spot[longest + 1:]
    return entries.at[tuple(spot)].set(low).at[tuple(next_to)].set(high)


def levels(own_key, shape, split, least, top_value):
    loudness = 1.0
    for dim, shards_of in split:
        draws = jax.random.uniform(jax.random.fold_in(jax.random.fold_in(own_key, 6), dim), (shards_of,), jnp.float32, least / len(split), top_value / len(split))
        loudness = loudness * jnp.repeat(jnp.exp(draws), shape[dim] // shards_of).reshape((-1,) + (1,) * (len(shape) - 1 - dim))
    return loudness


def setup_inputs(seed: int = 0) -> dict:
    seeds = jax.random.split(jax.random.key(seed), 4)
    return {
        "spins": with_ends((jax.random.randint(seeds[0], (NS, L), 0, 2) < 1).astype(jnp.int32), jax.random.fold_in(seeds[0], 1), 0, 1),
        "activations": jnp.clip(0.5 * jax.random.uniform(seeds[1], (PANELS, NS, L, A), jnp.float32) ** levels(seeds[1], (PANELS, NS, L, A), ((0, 4), (1, 8)), -0.2, 0.2), 0.0, 0.5),
        "gradients": jnp.clip(-0.1 + 0.4 * jax.random.uniform(seeds[2], (PANELS, NS, L, B), jnp.float32) ** levels(seeds[2], (PANELS, NS, L, B), ((0, 4), (1, 8)), -0.2, 0.2), -0.1, 0.3),
    }


def panel_scores(act, grad, occupied):
    weighted = act * occupied[:, :, None]
    score = jnp.einsum("sra,srb->sab", weighted, grad, precision=lax.Precision.HIGHEST)
    return score.reshape(score.shape[0], -1)


def reference(spins, activations, gradients):
    occupied = spins.astype(jnp.float32)
    gram = jnp.zeros((NS, NS), jnp.float32)
    for panel in range(PANELS):
        score = panel_scores(activations[panel], gradients[panel], occupied)
        centered = score - jnp.mean(score, axis=0, keepdims=True)
        gram = gram + jnp.dot(centered, centered.T, precision=lax.Precision.HIGHEST, preferred_element_type=jnp.float32)
    return gram / NS
```

```python
import functools

import jax
import jax.numpy as jnp
from jax import lax
from jax.experimental import pallas as pl
from jax.experimental.pallas import tpu as pltpu
from jax.sharding import PartitionSpec as P

LANES = 128


def score_kernel(pieces, spins_ref, act_ref, grad_ref, score_ref):
    occupied = spins_ref[...].astype(jnp.float32)
    weighted = act_ref[...].T * occupied
    score = jnp.dot(
        weighted,
        grad_ref[...],
        precision=lax.Precision.HIGHEST,
        preferred_element_type=jnp.float32,
    )
    rows = score.shape[0] // pieces
    parts = score.shape[1] // LANES
    for piece in range(pieces):
        for part in range(parts):
            score_ref[pl.ds((piece * parts + part) * rows, rows), :] = score[
                piece * rows : (piece + 1) * rows, part * LANES : (part + 1) * LANES
            ]


def gram_kernel(samples, copies, moved_ref, gram_ref):
    rows = moved_ref.shape[0] // samples
    gram = jnp.zeros((samples, samples), jnp.float32)
    for row in range(rows):
        score = moved_ref[pl.ds(row, samples, stride=rows), :]
        centered = score - jnp.sum(score, axis=0, keepdims=True) * (1.0 / samples)
        gram = gram + lax.dot_general(
            centered,
            centered,
            (((1,), (1,)), ((), ())),
            precision=lax.Precision.HIGHEST,
            preferred_element_type=jnp.float32,
        )
    gram = gram / samples
    for s in range(samples):
        gram_ref[pl.ds(s * copies, copies), pl.ds(0, samples)] = jnp.broadcast_to(gram[s : s + 1, :], (copies, samples))


def vmem(count):
    return [pl.BlockSpec(memory_space=pltpu.VMEM)] * count


def body(spins, activations, gradients):
    n_dev, n_rep = lax.axis_size("dev"), lax.axis_size("rep")
    act, grad = activations[0, 0], gradients[0, 0]
    channels, outputs = act.shape[1], grad.shape[1]
    score = pl.pallas_call(
        functools.partial(score_kernel, n_dev),
        out_shape=jax.ShapeDtypeStruct((channels * outputs // LANES, LANES), jnp.float32),
        in_specs=vmem(3),
        out_specs=vmem(1)[0],
        name="score",
    )(spins, act, grad)
    moved = lax.all_to_all(score, "dev", split_axis=0, concat_axis=0, tiled=True)
    partial = pl.pallas_call(
        functools.partial(gram_kernel, n_dev, n_rep),
        out_shape=jax.ShapeDtypeStruct((n_dev * n_rep, LANES), jnp.float32),
        in_specs=vmem(1),
        out_specs=vmem(1)[0],
        name="gram",
    )(moved)
    parts = lax.all_to_all(partial, ("dev", "rep"), split_axis=0, concat_axis=0, tiled=True)
    total = jnp.sum(parts, axis=0, keepdims=True)
    width = n_dev // n_rep
    return lax.dynamic_slice_in_dim(total, lax.axis_index("rep") * width, width, 1)


def solution(mesh):
    return jax.shard_map(
        body,
        mesh=mesh,
        in_specs=(P("dev", None), P("rep", "dev", None, None), P("rep", "dev", None, None)),
        out_specs=P("dev", "rep"),
        check_vma=False,
    )
```

```python
import functools

import jax
import jax.numpy as jnp
from jax import lax
from jax.experimental import pallas as pl
from jax.experimental.pallas import tpu as pltpu
from jax.sharding import PartitionSpec as P

LANES = 128
PARAMS = pltpu.CompilerParams(vmem_limit_bytes=4 * 1024 * 1024)
VMEM = pl.BlockSpec(memory_space=pltpu.VMEM)


def score_kernel(pieces, spins_hbm, act_hbm, grad_hbm, score_ref, spins_ref, act_ref, grad_ref, sems):
    copies = [
        pltpu.make_async_copy(src, dst, sems.at[i])
        for i, (src, dst) in enumerate(((grad_hbm, grad_ref), (act_hbm, act_ref), (spins_hbm, spins_ref)))
    ]
    for copy in copies:
        copy.start()
    for copy in copies:
        copy.wait()
    occupied = spins_ref[...].astype(jnp.float32)
    weighted = act_ref[...].T * occupied
    score = jnp.dot(
        weighted,
        grad_ref[...],
        precision=lax.Precision.HIGHEST,
        preferred_element_type=jnp.float32,
    )
    rows = score.shape[0] // pieces
    parts = score.shape[1] // LANES
    for piece in range(pieces):
        for part in range(parts):
            score_ref[pl.ds((piece * parts + part) * rows, rows), :] = score[
                piece * rows : (piece + 1) * rows, part * LANES : (part + 1) * LANES
            ]


def gram_kernel(samples, shares, moved_ref, gram_ref, wide_ref):
    rows = moved_ref.shape[0] // samples
    gram = jnp.zeros((samples, samples), jnp.float32)
    for row in range(rows):
        score = moved_ref[pl.ds(row, samples, stride=rows), :]
        centered = score - jnp.sum(score, axis=0, keepdims=True) * (1.0 / samples)
        gram = gram + lax.dot_general(
            centered,
            centered,
            (((1,), (1,)), ((), ())),
            precision=lax.Precision.HIGHEST,
            preferred_element_type=jnp.float32,
        )
    wide_ref[...] = jnp.zeros_like(wide_ref)
    wide_ref[:, pl.ds(0, samples)] = gram / samples
    wide = wide_ref[...]
    for share in range(shares):
        turned = wide if share == 0 else pltpu.roll(wide, LANES - share * (samples // shares), axis=1)
        gram_ref[pl.ds(share, samples, stride=shares), :] = turned


def body(spins, activations, gradients):
    n_dev, n_rep = lax.axis_size("dev"), lax.axis_size("rep")
    act, grad = activations[0, 0], gradients[0, 0]
    channels, outputs = act.shape[1], grad.shape[1]
    score = pl.pallas_call(
        functools.partial(score_kernel, n_dev),
        out_shape=jax.ShapeDtypeStruct((channels * outputs // LANES, LANES), jnp.float32),
        in_specs=[pl.BlockSpec(memory_space=pltpu.HBM)] * 3,
        out_specs=VMEM,
        scratch_shapes=[
            pltpu.VMEM(spins.shape, spins.dtype),
            pltpu.VMEM(act.shape, act.dtype),
            pltpu.VMEM(grad.shape, grad.dtype),
            pltpu.SemaphoreType.DMA((3,)),
        ],
        compiler_params=PARAMS,
        name="score",
    )(*(pltpu.with_memory_space_constraint(x, pltpu.HBM) for x in (spins, act, grad)))
    moved = lax.all_to_all(score, "dev", split_axis=0, concat_axis=0, tiled=True)
    partial = pl.pallas_call(
        functools.partial(gram_kernel, n_dev, n_rep),
        out_shape=jax.ShapeDtypeStruct((n_dev * n_rep, LANES), jnp.float32),
        in_specs=[VMEM],
        out_specs=VMEM,
        scratch_shapes=[pltpu.VMEM((n_dev, LANES), jnp.float32)],
        compiler_params=PARAMS,
        name="gram",
    )(moved)
    parts = lax.all_to_all(partial, ("dev", "rep"), split_axis=0, concat_axis=0, tiled=True)
    return jnp.sum(parts, axis=0, keepdims=True)[:, : n_dev // n_rep]


def solution(mesh):
    return jax.shard_map(
        body,
        mesh=mesh,
        in_specs=(P("dev", None), P("rep", "dev", None, None), P("rep", "dev", None, None)),
        out_specs=P("dev", "rep"),
        check_vma=False,
    )
```

```python
import functools

import jax
import jax.numpy as jnp
from jax import lax
from jax.experimental import pallas as pl
from jax.experimental.pallas import tpu as pltpu
from jax.sharding import PartitionSpec as P

LANES = 128
TERMS = 3
PARAMS = pltpu.CompilerParams(vmem_limit_bytes=4 * 1024 * 1024)
HBM = pl.BlockSpec(memory_space=pltpu.HBM)
VMEM = pl.BlockSpec(memory_space=pltpu.VMEM)
SMEM = pl.BlockSpec(memory_space=pltpu.SMEM)


def score_kernel(order, index_ref, spins_hbm, act_hbm, grad_hbm, index_out, score_ref, spins_ref, act_ref, grad_ref, sems):
    copies = [
        pltpu.make_async_copy(src, dst, sems.at[i])
        for i, (src, dst) in enumerate(((grad_hbm, grad_ref), (act_hbm, act_ref), (spins_hbm, spins_ref)))
    ]
    for copy in copies:
        copy.start()
    index_out[0] = index_ref[0]
    for copy in copies:
        copy.wait()
    occupied = spins_ref[...].astype(jnp.float32)
    weighted = act_ref[...].T * occupied
    score = jnp.dot(
        weighted,
        grad_ref[...],
        precision=lax.Precision.HIGHEST,
        preferred_element_type=jnp.float32,
    )
    slices = len(order) // 2
    rows = score.shape[0] // slices
    parts = score.shape[1] // LANES
    for place, owner in enumerate(order):
        piece = owner % slices
        for part in range(parts):
            score_ref[pl.ds((place * parts + part) * rows, rows), :] = score[
                piece * rows : (piece + 1) * rows, part * LANES : (part + 1) * LANES
            ]


def gram_kernel(order, goal, shares, index_ref, moved_ref, gram_ref, wide_ref):
    samples = len(order)
    rows = moved_ref.shape[0] // samples
    total = jnp.zeros((TERMS * samples, TERMS * samples), jnp.float32)
    for row in range(0, rows, 2):
        terms = []
        rest = []
        for step in range(2):
            score = moved_ref[pl.ds(row + step, samples, stride=rows), :]
            rest.append(score - jnp.sum(score, axis=0, keepdims=True) * (1.0 / samples))
        rest = jnp.concatenate(rest, axis=1)
        for _ in range(TERMS):
            term = rest.astype(jnp.bfloat16).astype(jnp.float32)
            terms.append(term)
            rest = rest - term
        stacked = jnp.concatenate(terms, axis=0).astype(jnp.bfloat16)
        total = total + lax.dot_general(
            stacked, stacked, (((1,), (1,)), ((), ())), preferred_element_type=jnp.float32
        )
    half = functools.reduce(jnp.add, [total[i * samples : (i + 1) * samples, :] for i in range(TERMS)])
    gram = functools.reduce(jnp.add, [half[:, i * samples : (i + 1) * samples] for i in range(TERMS)])
    wide_ref[...] = jnp.zeros_like(wide_ref)
    wide_ref[:, pl.ds(0, samples)] = gram / samples
    wide = wide_ref[...]
    width = samples // shares
    upper = index_ref[0] != 0
    members = len(goal)
    place = {owner: i for i, owner in enumerate(order)}
    for share in range(shares):
        column = place[share * width]
        turned = wide if column == 0 else pltpu.roll(wide, LANES - column, axis=1)
        for row in range(members // shares):
            low, high = place[row], place[row + members // shares]
            value = jnp.where(upper, turned[high : high + 1, :], turned[low : low + 1, :])
            gram_ref[pl.ds(goal.index(row * shares + share), 1), :] = value


def body(spins, activations, gradients):
    n_dev, n_rep = lax.axis_size("dev"), lax.axis_size("rep")
    act, grad = activations[0, 0], gradients[0, 0]
    channels, outputs = act.shape[1], grad.shape[1]
    width = n_dev // n_rep
    order = [place ^ (n_dev - width) for place in range(n_dev)]
    members = n_dev * n_rep // 2
    goal = [members - 1 - place for place in range(members)]
    size = channels * outputs // LANES // (n_dev // 2)
    index = (lax.axis_index("dev") // (n_dev // 2)).astype(jnp.int32).reshape(1)
    index, score = pl.pallas_call(
        functools.partial(score_kernel, order),
        out_shape=[
            jax.ShapeDtypeStruct((1,), jnp.int32),
            jax.ShapeDtypeStruct((n_dev * size, LANES), jnp.float32),
        ],
        in_specs=[SMEM, HBM, HBM, HBM],
        out_specs=[SMEM, VMEM],
        scratch_shapes=[
            pltpu.VMEM(spins.shape, spins.dtype),
            pltpu.VMEM(act.shape, act.dtype),
            pltpu.VMEM(grad.shape, grad.dtype),
            pltpu.SemaphoreType.DMA((3,)),
        ],
        compiler_params=PARAMS,
        name="score",
    )(index, *(pltpu.with_memory_space_constraint(x, pltpu.HBM) for x in (spins, act, grad)))
    moved = lax.all_to_all(score, "dev", split_axis=0, concat_axis=0, tiled=True, axis_index_groups=[order])
    partial = pl.pallas_call(
        functools.partial(gram_kernel, order, goal, n_rep),
        out_shape=jax.ShapeDtypeStruct((members, LANES), jnp.float32),
        in_specs=[SMEM, VMEM],
        out_specs=VMEM,
        scratch_shapes=[pltpu.VMEM((n_dev, LANES), jnp.float32)],
        compiler_params=PARAMS,
        name="gram",
    )(index, moved)
    groups = [[half * members + member for member in goal] for half in range(2)]
    parts = lax.all_to_all(
        partial, ("dev", "rep"), split_axis=0, concat_axis=0, tiled=True, axis_index_groups=groups
    )
    return jnp.sum(parts, axis=0, keepdims=True)[:, :width]


def solution(mesh):
    return jax.shard_map(
        body,
        mesh=mesh,
        in_specs=(P("dev", None), P("rep", "dev", None, None), P("rep", "dev", None, None)),
        out_specs=P("dev", "rep"),
        check_vma=False,
    )
```

```python
import functools

import jax
import jax.numpy as jnp
from jax import lax
from jax.experimental import pallas as pl
from jax.experimental.pallas import tpu as pltpu
from jax.sharding import PartitionSpec as P

LANES = 128
UNROLLED = 16
PARAMS = pltpu.CompilerParams(vmem_limit_bytes=8 * 1024 * 1024)
HBM = pl.BlockSpec(memory_space=pltpu.HBM)
VMEM = pl.BlockSpec(memory_space=pltpu.VMEM)
SMEM = pl.BlockSpec(memory_space=pltpu.SMEM)


def score_kernel(order, index_ref, spins_hbm, act_hbm, grad_hbm, score_ref, spins_ref, act_ref, grad_ref, sems):
    copies = [
        pltpu.make_async_copy(src, dst, sems.at[i])
        for i, (src, dst) in enumerate(((grad_hbm, grad_ref), (act_hbm, act_ref), (spins_hbm, spins_ref)))
    ]
    for copy in copies:
        copy.start()
    for copy in copies:
        copy.wait()
    occupied = spins_ref[...].astype(jnp.float32)
    weighted = act_ref[...].T * occupied
    score = jnp.dot(
        weighted,
        grad_ref[...],
        precision=lax.Precision.HIGHEST,
        preferred_element_type=jnp.float32,
    )
    slices = len(order) // 2
    rows = score.shape[0] // slices
    parts = score.shape[1] // LANES
    for place, owner in enumerate(order):
        piece = owner % slices
        for part in range(parts):
            score_ref[pl.ds((place * parts + part) * rows, rows), :] = score[
                piece * rows : (piece + 1) * rows, part * LANES : (part + 1) * LANES
            ]


def each(count, step):
    if count <= UNROLLED:
        for i in range(count):
            step(i)
    else:
        pl.loop(0, count)(step)


def gram_kernel(order, members, shares, index_ref, moved_ref, gram_ref, centered_ref, lanes_ref):
    samples = len(order)
    width = samples // shares
    rows = moved_ref.shape[0] // samples
    scores = [moved_ref[pl.ds(place * rows, rows), :] for place in range(samples)]
    mean = functools.reduce(jnp.add, scores) * (1.0 / samples)
    for place, owner in enumerate(order):
        centered_ref[owner] = scores[place] - mean
    mine = members // shares
    first = index_ref[0] * mine

    def row_step(row):
        own = centered_ref[first + row]
        for share in range(shares):
            def column_step(column):
                product = own * centered_ref[share * width + column]
                place = members - 1 - (row * shares + share)
                lanes_ref[column, pl.ds(place, 1), :] = jnp.sum(product, axis=0, keepdims=True)

            each(width, column_step)

    each(mine, row_step)
    lane = lax.broadcasted_iota(jnp.int32, (members, LANES), 1)
    gram = jnp.zeros((members, LANES), jnp.float32)
    for column in range(width):
        gram = jnp.where(lane == column, jnp.sum(lanes_ref[column], axis=1, keepdims=True), gram)
    gram_ref[...] = gram * (1.0 / samples)


def body(spins, activations, gradients):
    n_dev, n_rep = lax.axis_size("dev"), lax.axis_size("rep")
    act, grad = activations[0, 0], gradients[0, 0]
    channels, outputs = act.shape[1], grad.shape[1]
    width = n_dev // n_rep
    order = [place ^ (n_dev - width) for place in range(n_dev)]
    members = n_dev * n_rep // 2
    goal = [members - 1 - place for place in range(members)]
    size = channels * outputs // LANES // (n_dev // 2)
    index = (lax.axis_index("dev") // (n_dev // 2)).astype(jnp.int32).reshape(1)
    score = pl.pallas_call(
        functools.partial(score_kernel, order),
        out_shape=jax.ShapeDtypeStruct((n_dev * size, LANES), jnp.float32),
        in_specs=[SMEM, HBM, HBM, HBM],
        out_specs=VMEM,
        scratch_shapes=[
            pltpu.VMEM(spins.shape, spins.dtype),
            pltpu.VMEM(act.shape, act.dtype),
            pltpu.VMEM(grad.shape, grad.dtype),
            pltpu.SemaphoreType.DMA((3,)),
        ],
        compiler_params=PARAMS,
        name="score",
    )(index, *(pltpu.with_memory_space_constraint(x, pltpu.HBM) for x in (spins, act, grad)))
    moved = lax.all_to_all(score, "dev", split_axis=0, concat_axis=0, tiled=True, axis_index_groups=[order])
    partial = pl.pallas_call(
        functools.partial(gram_kernel, order, members, n_rep),
        out_shape=jax.ShapeDtypeStruct((members, LANES), jnp.float32),
        in_specs=[SMEM, VMEM],
        out_specs=VMEM,
        scratch_shapes=[
            pltpu.VMEM((n_dev, size, LANES), jnp.float32),
            pltpu.VMEM((width, members, LANES), jnp.float32),
        ],
        compiler_params=PARAMS,
        name="gram",
    )(index, moved)
    groups = [[half * members + member for member in goal] for half in range(2)]
    parts = lax.all_to_all(
        partial, ("dev", "rep"), split_axis=0, concat_axis=0, tiled=True, axis_index_groups=groups
    )
    return jnp.sum(parts, axis=0, keepdims=True)[:, :width]


def solution(mesh):
    return jax.shard_map(
        body,
        mesh=mesh,
        in_specs=(P("dev", None), P("rep", "dev", None, None), P("rep", "dev", None, None)),
        out_specs=P("dev", "rep"),
        check_vma=False,
    )
```

```python
import functools

import jax
import jax.numpy as jnp
from jax import lax
from jax.experimental import pallas as pl
from jax.experimental.pallas import tpu as pltpu
from jax.sharding import PartitionSpec as P

LANES = 128
UNROLLED = 16
TERMS = 3
PARAMS = pltpu.CompilerParams(vmem_limit_bytes=8 * 1024 * 1024)
HBM = pl.BlockSpec(memory_space=pltpu.HBM)
VMEM = pl.BlockSpec(memory_space=pltpu.VMEM)
SMEM = pl.BlockSpec(memory_space=pltpu.SMEM)


def terms(value):
    out = []
    for _ in range(TERMS):
        out.append(value.astype(jnp.bfloat16).astype(jnp.float32))
        value = value - out[-1]
    return out


def score_kernel(order, index_ref, spins_hbm, act_hbm, grad_hbm, score_ref, spins_ref, act_ref, grad_ref, sems):
    copies = [
        pltpu.make_async_copy(src, dst, sems.at[i])
        for i, (src, dst) in enumerate(((grad_hbm, grad_ref), (act_hbm, act_ref), (spins_hbm, spins_ref)))
    ]
    for copy in copies:
        copy.start()
    for copy in copies:
        copy.wait()
    occupied = spins_ref[...].astype(jnp.float32)
    act, grad = terms(act_ref[...]), terms(grad_ref[...])
    pairs = [(i, j) for i in range(TERMS) for j in range(TERMS - i)]
    weighted = jnp.concatenate([act[i] for i, _ in pairs], axis=0).T * jnp.concatenate([occupied] * len(pairs), axis=1)
    score = jnp.dot(
        weighted.astype(jnp.bfloat16),
        jnp.concatenate([grad[j] for _, j in pairs], axis=0).astype(jnp.bfloat16),
        preferred_element_type=jnp.float32,
    )
    slices = len(order) // 2
    rows = score.shape[0] // slices
    parts = score.shape[1] // LANES
    for place, owner in enumerate(order):
        piece = owner % slices
        for part in range(parts):
            score_ref[pl.ds((place * parts + part) * rows, rows), :] = score[
                piece * rows : (piece + 1) * rows, part * LANES : (part + 1) * LANES
            ]


def each(count, step):
    if count <= UNROLLED:
        for i in range(count):
            step(i)
    else:
        pl.loop(0, count)(step)


def gram_kernel(order, members, shares, index_ref, moved_ref, gram_ref, centered_ref, lanes_ref):
    samples = len(order)
    width = samples // shares
    rows = moved_ref.shape[0] // samples
    scores = [moved_ref[pl.ds(place * rows, rows), :] for place in range(samples)]
    mean = functools.reduce(jnp.add, scores) * (1.0 / samples)
    for place, owner in enumerate(order):
        centered_ref[owner] = scores[place] - mean
    mine = members // shares
    first = index_ref[0] * mine

    def row_step(row):
        own = centered_ref[first + row]
        for share in range(shares):
            def column_step(column):
                product = own * centered_ref[share * width + column]
                place = members - 1 - (row * shares + share)
                lanes_ref[column, pl.ds(place, 1), :] = jnp.sum(product, axis=0, keepdims=True)

            each(width, column_step)

    each(mine, row_step)
    lane = lax.broadcasted_iota(jnp.int32, (members, LANES), 1)
    gram = jnp.zeros((members, LANES), jnp.float32)
    for column in range(width):
        gram = jnp.where(lane == column, jnp.sum(lanes_ref[column], axis=1, keepdims=True), gram)
    gram_ref[...] = gram * (1.0 / samples)


def body(spins, activations, gradients):
    n_dev, n_rep = lax.axis_size("dev"), lax.axis_size("rep")
    act, grad = activations[0, 0], gradients[0, 0]
    channels, outputs = act.shape[1], grad.shape[1]
    width = n_dev // n_rep
    order = [2 * (i ^ (i >> 1) ^ (n_dev // 4)) + j for j in (1, 0) for i in range(n_dev // 2)]
    members = n_dev * n_rep // 2
    goal = [members - 1 - place for place in range(members)]
    size = channels * outputs // LANES // (n_dev // 2)
    index = (lax.axis_index("dev") // (n_dev // 2)).astype(jnp.int32).reshape(1)
    score = pl.pallas_call(
        functools.partial(score_kernel, order),
        out_shape=jax.ShapeDtypeStruct((n_dev * size, LANES), jnp.float32),
        in_specs=[SMEM, HBM, HBM, HBM],
        out_specs=VMEM,
        scratch_shapes=[
            pltpu.VMEM(spins.shape, spins.dtype),
            pltpu.VMEM(act.shape, act.dtype),
            pltpu.VMEM(grad.shape, grad.dtype),
            pltpu.SemaphoreType.DMA((3,)),
        ],
        compiler_params=PARAMS,
        name="score",
    )(index, *(pltpu.with_memory_space_constraint(x, pltpu.HBM) for x in (spins, act, grad)))
    moved = lax.all_to_all(score, "dev", split_axis=0, concat_axis=0, tiled=True, axis_index_groups=[order])
    partial = pl.pallas_call(
        functools.partial(gram_kernel, order, members, n_rep),
        out_shape=jax.ShapeDtypeStruct((members, LANES), jnp.float32),
        in_specs=[SMEM, VMEM],
        out_specs=VMEM,
        scratch_shapes=[
            pltpu.VMEM((n_dev, size, LANES), jnp.float32),
            pltpu.VMEM((width, members, LANES), jnp.float32),
        ],
        compiler_params=PARAMS,
        name="gram",
    )(index, moved)
    groups = [[half * members + member for member in goal] for half in range(2)]
    parts = lax.all_to_all(
        partial, ("dev", "rep"), split_axis=0, concat_axis=0, tiled=True, axis_index_groups=groups
    )
    return jnp.sum(parts, axis=0, keepdims=True)[:, :width]


def solution(mesh):
    return jax.shard_map(
        body,
        mesh=mesh,
        in_specs=(P("dev", None), P("rep", "dev", None, None), P("rep", "dev", None, None)),
        out_specs=P("dev", "rep"),
        check_vma=False,
    )
```

```python
import functools

import jax
import jax.numpy as jnp
from jax import lax
from jax.experimental import pallas as pl
from jax.experimental.pallas import tpu as pltpu
from jax.sharding import PartitionSpec as P

LANES = 128
UNROLLED = 16
TERMS = 3
PARAMS = pltpu.CompilerParams(vmem_limit_bytes=8 * 1024 * 1024)
HBM = pl.BlockSpec(memory_space=pltpu.HBM)
VMEM = pl.BlockSpec(memory_space=pltpu.VMEM)
SMEM = pl.BlockSpec(memory_space=pltpu.SMEM)


def terms(value):
    out = []
    for _ in range(TERMS):
        out.append(value.astype(jnp.bfloat16).astype(jnp.float32))
        value = value - out[-1]
    return out


def score_kernel(order, index_ref, spins_hbm, act_hbm, grad_hbm, score_ref, spins_ref, act_ref, grad_ref, sems):
    half = grad_hbm.shape[0] // 2
    copies = [
        pltpu.make_async_copy(src, dst, sems.at[i])
        for i, (src, dst) in enumerate((
            (grad_hbm.at[pl.ds(0, half)], grad_ref.at[pl.ds(0, half)]),
            (grad_hbm.at[pl.ds(half, half)], grad_ref.at[pl.ds(half, half)]),
            (act_hbm, act_ref), (spins_hbm, spins_ref)))
    ]
    for copy in copies:
        copy.start()
    for copy in copies:
        copy.wait()
    occupied = spins_ref[...].astype(jnp.bfloat16)
    act, grad = terms(act_ref[...]), terms(grad_ref[...])
    pairs = [(i, j) for i in range(TERMS) for j in range(TERMS - i)]
    weighted = jnp.concatenate([act[i].astype(jnp.bfloat16) for i, _ in pairs], axis=0).T
    weighted = weighted * jnp.concatenate([occupied] * len(pairs), axis=1)
    score = jnp.dot(
        weighted,
        jnp.concatenate([grad[j].astype(jnp.bfloat16) for _, j in pairs], axis=0),
        preferred_element_type=jnp.float32,
    )
    slices = len(order) // 2
    rows = score.shape[0] // slices
    parts = score.shape[1] // LANES
    for place, owner in enumerate(order):
        piece = owner % slices
        for part in range(parts):
            score_ref[pl.ds((place * parts + part) * rows, rows), :] = score[
                piece * rows : (piece + 1) * rows, part * LANES : (part + 1) * LANES
            ]


def each(count, step):
    if count <= UNROLLED:
        for i in range(count):
            step(i)
    else:
        pl.loop(0, count)(step)


def gram_kernel(order, members, shares, index_ref, moved_ref, gram_ref, centered_ref, lanes_ref):
    samples = len(order)
    width = samples // shares
    rows = moved_ref.shape[0] // samples
    scores = [moved_ref[pl.ds(place * rows, rows), :] for place in range(samples)]
    mean = functools.reduce(jnp.add, scores) * (1.0 / samples)
    for place, owner in enumerate(order):
        centered_ref[owner] = scores[place] - mean
    mine = members // shares
    first = index_ref[0] * mine

    def row_step(row):
        own = centered_ref[first + row]
        for share in range(shares):
            def column_step(column):
                product = own * centered_ref[share * width + column]
                place = members - 1 - (row * shares + share)
                lanes_ref[column, pl.ds(place, 1), :] = jnp.sum(product, axis=0, keepdims=True)

            each(width, column_step)

    each(mine, row_step)
    lane = lax.broadcasted_iota(jnp.int32, (members, LANES), 1)
    gram = jnp.zeros((members, LANES), jnp.float32)
    for column in range(width):
        gram = jnp.where(lane == column, jnp.sum(lanes_ref[column], axis=1, keepdims=True), gram)
    gram_ref[...] = gram * (1.0 / samples)


def body(spins, activations, gradients):
    n_dev, n_rep = lax.axis_size("dev"), lax.axis_size("rep")
    act, grad = activations[0, 0], gradients[0, 0]
    channels, outputs = act.shape[1], grad.shape[1]
    width = n_dev // n_rep
    order = [2 * (i ^ (i >> 1) ^ (n_dev // 4)) + j for j in (1, 0) for i in range(n_dev // 2)]
    members = n_dev * n_rep // 2
    goal = [members - 1 - place for place in range(members)]
    size = channels * outputs // LANES // (n_dev // 2)
    index = (lax.axis_index("dev") // (n_dev // 2)).astype(jnp.int32).reshape(1)
    score = pl.pallas_call(
        functools.partial(score_kernel, order),
        out_shape=jax.ShapeDtypeStruct((n_dev * size, LANES), jnp.float32),
        in_specs=[SMEM, HBM, HBM, HBM],
        out_specs=VMEM,
        scratch_shapes=[
            pltpu.VMEM(spins.shape, spins.dtype),
            pltpu.VMEM(act.shape, act.dtype),
            pltpu.VMEM(grad.shape, grad.dtype),
            pltpu.SemaphoreType.DMA((4,)),
        ],
        compiler_params=PARAMS,
        name="score",
    )(index, *(pltpu.with_memory_space_constraint(x, pltpu.HBM) for x in (spins, act, grad)))
    moved = lax.all_to_all(score, "dev", split_axis=0, concat_axis=0, tiled=True, axis_index_groups=[order])
    partial = pl.pallas_call(
        functools.partial(gram_kernel, order, members, n_rep),
        out_shape=jax.ShapeDtypeStruct((members, LANES), jnp.float32),
        in_specs=[SMEM, VMEM],
        out_specs=VMEM,
        scratch_shapes=[
            pltpu.VMEM((n_dev, size, LANES), jnp.float32),
            pltpu.VMEM((width, members, LANES), jnp.float32),
        ],
        compiler_params=PARAMS,
        name="gram",
    )(index, moved)
    groups = [[half * members + member for member in goal] for half in range(2)]
    parts = lax.all_to_all(
        partial, ("dev", "rep"), split_axis=0, concat_axis=0, tiled=True, axis_index_groups=groups
    )
    return jnp.sum(parts, axis=0, keepdims=True)[:, :width]


def solution(mesh):
    return jax.shard_map(
        body,
        mesh=mesh,
        in_specs=(P("dev", None), P("rep", "dev", None, None), P("rep", "dev", None, None)),
        out_specs=P("dev", "rep"),
        check_vma=False,
    )
```

```python
import functools

import jax
import jax.numpy as jnp
from jax import lax
from jax.experimental import pallas as pl
from jax.experimental.pallas import tpu as pltpu
from jax.sharding import PartitionSpec as P

LANES = 128
UNROLLED = 16
TERMS = 3
PARAMS = pltpu.CompilerParams(vmem_limit_bytes=8 * 1024 * 1024)
HBM = pl.BlockSpec(memory_space=pltpu.HBM)
VMEM = pl.BlockSpec(memory_space=pltpu.VMEM)
SMEM = pl.BlockSpec(memory_space=pltpu.SMEM)


def terms(value):
    out = []
    for _ in range(TERMS):
        out.append(value.astype(jnp.bfloat16).astype(jnp.float32))
        value = value - out[-1]
    return out


def score_kernel(orders, index_ref, spins_hbm, act_hbm, grad_hbm, score_ref, spins_ref, act_ref, grad_ref, sems):
    copies = [
        pltpu.make_async_copy(src, dst, sems.at[i])
        for i, (src, dst) in enumerate(((grad_hbm, grad_ref), (act_hbm, act_ref), (spins_hbm, spins_ref)))
    ]
    for copy in copies:
        copy.start()
    for copy in copies:
        copy.wait()
    occupied = spins_ref[...].astype(jnp.float32)
    act, grad = terms(act_ref[...]), terms(grad_ref[...])
    pairs = [(i, j) for i in range(TERMS) for j in range(TERMS - i)]
    weighted = jnp.concatenate([act[i] for i, _ in pairs], axis=0).T * jnp.concatenate([occupied] * len(pairs), axis=1)
    score = jnp.dot(
        weighted.astype(jnp.bfloat16),
        jnp.concatenate([grad[j] for _, j in pairs], axis=0).astype(jnp.bfloat16),
        preferred_element_type=jnp.float32,
    )
    slices = len(orders[0]) // 2
    rows = score.shape[0] // slices
    parts = score.shape[1] // LANES
    odd = index_ref[0] % 2 != 0
    for place, owners in enumerate(zip(*orders)):
        pieces = [owner % slices for owner in owners]
        blocks = [score[piece * rows : (piece + 1) * rows, :] for piece in pieces]
        block = blocks[0] if pieces[0] == pieces[1] else jnp.where(odd, blocks[1], blocks[0])
        for part in range(parts):
            score_ref[pl.ds((place * parts + part) * rows, rows), :] = block[:, part * LANES : (part + 1) * LANES]


def each(count, step):
    if count <= UNROLLED:
        for i in range(count):
            step(i)
    else:
        pl.loop(0, count)(step)


def gram_kernel(orders, members, shares, index_ref, moved_ref, gram_ref, centered_ref, lanes_ref):
    samples = len(orders[0])
    odd = index_ref[0] % 2 != 0
    width = samples // shares
    rows = moved_ref.shape[0] // samples
    scores = [moved_ref[pl.ds(place * rows, rows), :] for place in range(samples)]
    mean = functools.reduce(jnp.add, scores) * (1.0 / samples)
    for place, (even_owner, odd_owner) in enumerate(zip(*orders)):
        centered_ref[jnp.where(odd, odd_owner, even_owner)] = scores[place] - mean
    mine = members // shares
    first = index_ref[0] // 2 * mine

    def row_step(row):
        own = centered_ref[first + row]
        for share in range(shares):
            def column_step(column):
                product = own * centered_ref[share * width + column]
                place = members - 1 - (row * shares + share)
                lanes_ref[column, pl.ds(place, 1), :] = jnp.sum(product, axis=0, keepdims=True)

            each(width, column_step)

    each(mine, row_step)
    lane = lax.broadcasted_iota(jnp.int32, (members, LANES), 1)
    gram = jnp.zeros((members, LANES), jnp.float32)
    for column in range(width):
        gram = jnp.where(lane == column, jnp.sum(lanes_ref[column], axis=1, keepdims=True), gram)
    gram_ref[...] = gram * (1.0 / samples)


def body(spins, activations, gradients):
    n_dev, n_rep = lax.axis_size("dev"), lax.axis_size("rep")
    act, grad = activations[0, 0], gradients[0, 0]
    channels, outputs = act.shape[1], grad.shape[1]
    width = n_dev // n_rep
    layers = n_dev // 2
    orders = [
        [2 * layer + j for j in (1, 0) for layer in along]
        for along in (
            [i ^ (i >> 1) ^ (layers // 2) for i in range(layers)],
            [(layers // 2 - i) % layers for i in range(layers)],
        )
    ]
    members = n_dev * n_rep // 2
    goal = [members - 1 - place for place in range(members)]
    size = channels * outputs // LANES // (n_dev // 2)
    index = (lax.axis_index("dev") // (n_dev // 2) * 2 + lax.axis_index("rep") % 2).astype(jnp.int32).reshape(1)
    score = pl.pallas_call(
        functools.partial(score_kernel, orders),
        out_shape=jax.ShapeDtypeStruct((n_dev * size, LANES), jnp.float32),
        in_specs=[SMEM, HBM, HBM, HBM],
        out_specs=VMEM,
        scratch_shapes=[
            pltpu.VMEM(spins.shape, spins.dtype),
            pltpu.VMEM(act.shape, act.dtype),
            pltpu.VMEM(grad.shape, grad.dtype),
            pltpu.SemaphoreType.DMA((3,)),
        ],
        compiler_params=PARAMS,
        name="score",
    )(index, *(pltpu.with_memory_space_constraint(x, pltpu.HBM) for x in (spins, act, grad)))
    columns = [[d * n_rep + r for d in orders[r % 2]] for r in range(n_rep)]
    moved = lax.all_to_all(
        score, ("dev", "rep"), split_axis=0, concat_axis=0, tiled=True, axis_index_groups=columns
    )
    partial = pl.pallas_call(
        functools.partial(gram_kernel, orders, members, n_rep),
        out_shape=jax.ShapeDtypeStruct((members, LANES), jnp.float32),
        in_specs=[SMEM, VMEM],
        out_specs=VMEM,
        scratch_shapes=[
            pltpu.VMEM((n_dev, size, LANES), jnp.float32),
            pltpu.VMEM((width, members, LANES), jnp.float32),
        ],
        compiler_params=PARAMS,
        name="gram",
    )(index, moved)
    groups = [[half * members + member for member in goal] for half in range(2)]
    parts = lax.all_to_all(
        partial, ("dev", "rep"), split_axis=0, concat_axis=0, tiled=True, axis_index_groups=groups
    )
    return jnp.sum(parts, axis=0, keepdims=True)[:, :width]


def solution(mesh):
    return jax.shard_map(
        body,
        mesh=mesh,
        in_specs=(P("dev", None), P("rep", "dev", None, None), P("rep", "dev", None, None)),
        out_specs=P("dev", "rep"),
        check_vma=False,
    )
```

```python
import functools

import jax
import jax.numpy as jnp
from jax import lax
from jax.experimental import pallas as pl
from jax.experimental.pallas import tpu as pltpu
from jax.sharding import PartitionSpec as P

LANES = 128
UNROLLED = 16
TERMS = 3
PARAMS = pltpu.CompilerParams(vmem_limit_bytes=8 * 1024 * 1024)
HBM = pl.BlockSpec(memory_space=pltpu.HBM)
VMEM = pl.BlockSpec(memory_space=pltpu.VMEM)
SMEM = pl.BlockSpec(memory_space=pltpu.SMEM)


def terms(value):
    out = []
    for _ in range(TERMS):
        out.append(value.astype(jnp.bfloat16).astype(jnp.float32))
        value = value - out[-1]
    return out


def score_kernel(orders, index_ref, spins_hbm, act_hbm, grad_hbm, score_ref, spins_ref, act_ref, grad_ref, sems):
    half = grad_hbm.shape[0] // 2
    copies = [
        pltpu.make_async_copy(src, dst, sems.at[i])
        for i, (src, dst) in enumerate((
            (grad_hbm.at[pl.ds(0, half)], grad_ref.at[pl.ds(0, half)]),
            (grad_hbm.at[pl.ds(half, half)], grad_ref.at[pl.ds(half, half)]),
            (act_hbm, act_ref), (spins_hbm, spins_ref)))
    ]
    for copy in copies:
        copy.start()
    for copy in copies:
        copy.wait()
    occupied = spins_ref[...].astype(jnp.bfloat16)
    act, grad = terms(act_ref[...]), terms(grad_ref[...])
    pairs = [(i, j) for i in range(TERMS) for j in range(TERMS - i)]
    weighted = jnp.concatenate([act[i].astype(jnp.bfloat16) for i, _ in pairs], axis=0).T
    weighted = weighted * jnp.concatenate([occupied] * len(pairs), axis=1)
    score = jnp.dot(
        weighted,
        jnp.concatenate([grad[j].astype(jnp.bfloat16) for _, j in pairs], axis=0),
        preferred_element_type=jnp.float32,
    )
    slices = len(orders[0]) // 2
    rows = score.shape[0] // slices
    parts = score.shape[1] // LANES
    odd = index_ref[0] % 2 != 0
    for place, owners in enumerate(zip(*orders)):
        pieces = [owner % slices for owner in owners]
        blocks = [score[piece * rows : (piece + 1) * rows, :] for piece in pieces]
        block = blocks[0] if pieces[0] == pieces[1] else jnp.where(odd, blocks[1], blocks[0])
        for part in range(parts):
            score_ref[pl.ds((place * parts + part) * rows, rows), :] = block[:, part * LANES : (part + 1) * LANES]


def each(count, step):
    if count <= UNROLLED:
        for i in range(count):
            step(i)
    else:
        pl.loop(0, count)(step)


def gram_kernel(orders, members, shares, index_ref, moved_ref, gram_ref, centered_ref, lanes_ref):
    samples = len(orders[0])
    odd = index_ref[0] % 2 != 0
    width = samples // shares
    rows = moved_ref.shape[0] // samples
    scores = [moved_ref[pl.ds(place * rows, rows), :] for place in range(samples)]
    mean = functools.reduce(jnp.add, scores) * (1.0 / samples)
    for place, (even_owner, odd_owner) in enumerate(zip(*orders)):
        centered_ref[jnp.where(odd, odd_owner, even_owner)] = scores[place] - mean
    mine = members // shares
    first = index_ref[0] // 2 * mine

    def row_step(row):
        own = centered_ref[first + row]
        for share in range(shares):
            def column_step(column):
                product = own * centered_ref[share * width + column]
                place = members - 1 - (row * shares + share)
                lanes_ref[column, pl.ds(place, 1), :] = jnp.sum(product, axis=0, keepdims=True)

            each(width, column_step)

    each(mine, row_step)
    lane = lax.broadcasted_iota(jnp.int32, (members, LANES), 1)
    gram = jnp.zeros((members, LANES), jnp.float32)
    for column in range(width):
        gram = jnp.where(lane == column, jnp.sum(lanes_ref[column], axis=1, keepdims=True), gram)
    gram_ref[...] = gram * (1.0 / samples)


def body(spins, activations, gradients):
    n_dev, n_rep = lax.axis_size("dev"), lax.axis_size("rep")
    act, grad = activations[0, 0], gradients[0, 0]
    channels, outputs = act.shape[1], grad.shape[1]
    width = n_dev // n_rep
    layers = n_dev // 2
    orders = [
        [2 * layer + j for j in (1, 0) for layer in along]
        for along in (
            [i ^ (i >> 1) ^ (layers // 2) for i in range(layers)],
            [(layers // 2 - i) % layers for i in range(layers)],
        )
    ]
    members = n_dev * n_rep // 2
    goal = [members - 1 - place for place in range(members)]
    size = channels * outputs // LANES // (n_dev // 2)
    index = (lax.axis_index("dev") // (n_dev // 2) * 2 + lax.axis_index("rep") % 2).astype(jnp.int32).reshape(1)
    score = pl.pallas_call(
        functools.partial(score_kernel, orders),
        out_shape=jax.ShapeDtypeStruct((n_dev * size, LANES), jnp.float32),
        in_specs=[SMEM, HBM, HBM, HBM],
        out_specs=VMEM,
        scratch_shapes=[
            pltpu.VMEM(spins.shape, spins.dtype),
            pltpu.VMEM(act.shape, act.dtype),
            pltpu.VMEM(grad.shape, grad.dtype),
            pltpu.SemaphoreType.DMA((4,)),
        ],
        compiler_params=PARAMS,
        name="score",
    )(index, *(pltpu.with_memory_space_constraint(x, pltpu.HBM) for x in (spins, act, grad)))
    columns = [[d * n_rep + r for d in orders[r % 2]] for r in range(n_rep)]
    moved = lax.all_to_all(
        score, ("dev", "rep"), split_axis=0, concat_axis=0, tiled=True, axis_index_groups=columns
    )
    partial = pl.pallas_call(
        functools.partial(gram_kernel, orders, members, n_rep),
        out_shape=jax.ShapeDtypeStruct((members, LANES), jnp.float32),
        in_specs=[SMEM, VMEM],
        out_specs=VMEM,
        scratch_shapes=[
            pltpu.VMEM((n_dev, size, LANES), jnp.float32),
            pltpu.VMEM((width, members, LANES), jnp.float32),
        ],
        compiler_params=PARAMS,
        name="gram",
    )(index, moved)
    groups = [[half * members + member for member in goal] for half in range(2)]
    parts = lax.all_to_all(
        partial, ("dev", "rep"), split_axis=0, concat_axis=0, tiled=True, axis_index_groups=groups
    )
    return jnp.sum(parts, axis=0, keepdims=True)[:, :width]


def solution(mesh):
    return jax.shard_map(
        body,
        mesh=mesh,
        in_specs=(P("dev", None), P("rep", "dev", None, None), P("rep", "dev", None, None)),
        out_specs=P("dev", "rep"),
        check_vma=False,
    )
```

```python
import functools

import jax
import jax.numpy as jnp
from jax import lax
from jax.experimental import pallas as pl
from jax.experimental.pallas import tpu as pltpu
from jax.sharding import PartitionSpec as P

LANES = 128
UNROLLED = 16
TERMS = 3
PARAMS = pltpu.CompilerParams(vmem_limit_bytes=8 * 1024 * 1024)
HBM = pl.BlockSpec(memory_space=pltpu.HBM)
VMEM = pl.BlockSpec(memory_space=pltpu.VMEM)
SMEM = pl.BlockSpec(memory_space=pltpu.SMEM)


def terms(value):
    out = []
    for _ in range(TERMS):
        out.append(value.astype(jnp.bfloat16).astype(jnp.float32))
        value = value - out[-1]
    return out


def score_kernel(orders, index_ref, spins_hbm, act_hbm, grad_hbm, score_ref, spins_ref, act_ref, grad_ref, sems):
    half = grad_hbm.shape[0] // 2
    copies = [
        pltpu.make_async_copy(src, dst, sems.at[i])
        for i, (src, dst) in enumerate((
            (grad_hbm.at[pl.ds(0, half)], grad_ref.at[pl.ds(0, half)]),
            (grad_hbm.at[pl.ds(half, half)], grad_ref.at[pl.ds(half, half)]),
            (act_hbm, act_ref), (spins_hbm, spins_ref)))
    ]
    for copy in copies:
        copy.start()
    for copy in copies[2:]:
        copy.wait()
    occupied = spins_ref[...].astype(jnp.bfloat16)
    act = terms(act_ref[...])
    pairs = [(i, j) for i in range(TERMS) for j in range(TERMS - i)]
    weighted = jnp.concatenate([act[i].astype(jnp.bfloat16) for i, _ in pairs], axis=0).T
    weighted = weighted * jnp.concatenate([occupied] * len(pairs), axis=1)
    for copy in copies[:2]:
        copy.wait()
    grad = terms(grad_ref[...])
    score = jnp.dot(
        weighted,
        jnp.concatenate([grad[j].astype(jnp.bfloat16) for _, j in pairs], axis=0),
        preferred_element_type=jnp.float32,
    )
    slices = len(orders[0]) // 2
    rows = score.shape[0] // slices
    parts = score.shape[1] // LANES
    odd = index_ref[0] % 2 != 0
    for place, owners in enumerate(zip(*orders)):
        pieces = [owner % slices for owner in owners]
        blocks = [score[piece * rows : (piece + 1) * rows, :] for piece in pieces]
        block = blocks[0] if pieces[0] == pieces[1] else jnp.where(odd, blocks[1], blocks[0])
        for part in range(parts):
            score_ref[pl.ds((place * parts + part) * rows, rows), :] = block[:, part * LANES : (part + 1) * LANES]


def each(count, step):
    if count <= UNROLLED:
        for i in range(count):
            step(i)
    else:
        pl.loop(0, count)(step)


def gram_kernel(orders, members, shares, index_ref, moved_ref, gram_ref, centered_ref, lanes_ref):
    samples = len(orders[0])
    odd = index_ref[0] % 2 != 0
    width = samples // shares
    rows = moved_ref.shape[0] // samples
    scores = [moved_ref[pl.ds(place * rows, rows), :] for place in range(samples)]
    mean = functools.reduce(jnp.add, scores) * (1.0 / samples)
    for place, (even_owner, odd_owner) in enumerate(zip(*orders)):
        centered_ref[jnp.where(odd, odd_owner, even_owner)] = scores[place] - mean
    mine = members // shares
    first = index_ref[0] // 2 * mine

    def row_step(row):
        own = centered_ref[first + row]
        for share in range(shares):
            def column_step(column):
                product = own * centered_ref[share * width + column]
                place = members - 1 - (row * shares + share)
                lanes_ref[column, pl.ds(place, 1), :] = jnp.sum(product, axis=0, keepdims=True)

            each(width, column_step)

    each(mine, row_step)
    lane = lax.broadcasted_iota(jnp.int32, (members, LANES), 1)
    gram = jnp.zeros((members, LANES), jnp.float32)
    for column in range(width):
        gram = jnp.where(lane == column, jnp.sum(lanes_ref[column], axis=1, keepdims=True), gram)
    gram_ref[...] = gram * (1.0 / samples)


def body(spins, activations, gradients):
    n_dev, n_rep = lax.axis_size("dev"), lax.axis_size("rep")
    act, grad = activations[0, 0], gradients[0, 0]
    channels, outputs = act.shape[1], grad.shape[1]
    width = n_dev // n_rep
    layers = n_dev // 2
    orders = [
        [2 * layer + j for j in (1, 0) for layer in along]
        for along in (
            [i ^ (i >> 1) ^ (layers // 2) for i in range(layers)],
            [(layers // 2 - i) % layers for i in range(layers)],
        )
    ]
    members = n_dev * n_rep // 2
    goal = [members - 1 - place for place in range(members)]
    size = channels * outputs // LANES // (n_dev // 2)
    index = (lax.axis_index("dev") // (n_dev // 2) * 2 + lax.axis_index("rep") % 2).astype(jnp.int32).reshape(1)
    score = pl.pallas_call(
        functools.partial(score_kernel, orders),
        out_shape=jax.ShapeDtypeStruct((n_dev * size, LANES), jnp.float32),
        in_specs=[SMEM, HBM, HBM, HBM],
        out_specs=VMEM,
        scratch_shapes=[
            pltpu.VMEM(spins.shape, spins.dtype),
            pltpu.VMEM(act.shape, act.dtype),
            pltpu.VMEM(grad.shape, grad.dtype),
            pltpu.SemaphoreType.DMA((4,)),
        ],
        compiler_params=PARAMS,
        name="score",
    )(index, *(pltpu.with_memory_space_constraint(x, pltpu.HBM) for x in (spins, act, grad)))
    columns = [[d * n_rep + r for d in orders[r % 2]] for r in range(n_rep)]
    moved = lax.all_to_all(
        score, ("dev", "rep"), split_axis=0, concat_axis=0, tiled=True, axis_index_groups=columns
    )
    partial = pl.pallas_call(
        functools.partial(gram_kernel, orders, members, n_rep),
        out_shape=jax.ShapeDtypeStruct((members, LANES), jnp.float32),
        in_specs=[SMEM, VMEM],
        out_specs=VMEM,
        scratch_shapes=[
            pltpu.VMEM((n_dev, size, LANES), jnp.float32),
            pltpu.VMEM((width, members, LANES), jnp.float32),
        ],
        compiler_params=PARAMS,
        name="gram",
    )(index, moved)
    groups = [[half * members + member for member in goal] for half in range(2)]
    parts = lax.all_to_all(
        partial, ("dev", "rep"), split_axis=0, concat_axis=0, tiled=True, axis_index_groups=groups
    )
    return jnp.sum(parts, axis=0, keepdims=True)[:, :width]


def solution(mesh):
    return jax.shard_map(
        body,
        mesh=mesh,
        in_specs=(P("dev", None), P("rep", "dev", None, None), P("rep", "dev", None, None)),
        out_specs=P("dev", "rep"),
        check_vma=False,
    )
```

```python
import functools

import jax
import jax.numpy as jnp
from jax import lax
from jax.experimental import pallas as pl
from jax.experimental.pallas import tpu as pltpu
from jax.sharding import PartitionSpec as P

LANES = 128
UNROLLED = 16
TERMS = 3
PARAMS = pltpu.CompilerParams(vmem_limit_bytes=8 * 1024 * 1024)
HBM = pl.BlockSpec(memory_space=pltpu.HBM)
VMEM = pl.BlockSpec(memory_space=pltpu.VMEM)
SMEM = pl.BlockSpec(memory_space=pltpu.SMEM)


def terms(value):
    out = []
    for _ in range(TERMS):
        out.append(value.astype(jnp.bfloat16).astype(jnp.float32))
        value = value - out[-1]
    return out


def score_kernel(orders, index_ref, spins_hbm, act_hbm, grad_hbm, score_ref, spins_ref, act_ref, grad_ref, sems):
    half = grad_hbm.shape[0] // 2
    copies = [
        pltpu.make_async_copy(src, dst, sems.at[i])
        for i, (src, dst) in enumerate((
            (grad_hbm.at[pl.ds(0, half)], grad_ref.at[pl.ds(0, half)]),
            (grad_hbm.at[pl.ds(half, half)], grad_ref.at[pl.ds(half, half)]),
            (act_hbm, act_ref), (spins_hbm, spins_ref)))
    ]
    for copy in copies[2:] + copies[:2]:
        copy.start()
    for copy in copies[2:]:
        copy.wait()
    occupied = spins_ref[...].astype(jnp.bfloat16)
    act = terms(act_ref[...])
    pairs = [(i, j) for i in range(TERMS) for j in range(TERMS - i)]
    weighted = jnp.concatenate([act[i].astype(jnp.bfloat16) for i, _ in pairs], axis=0).T
    weighted = weighted * jnp.concatenate([occupied] * len(pairs), axis=1)
    for copy in copies[:2]:
        copy.wait()
    grad = terms(grad_ref[...])
    score = jnp.dot(
        weighted,
        jnp.concatenate([grad[j].astype(jnp.bfloat16) for _, j in pairs], axis=0),
        preferred_element_type=jnp.float32,
    )
    slices = len(orders[0]) // 2
    rows = score.shape[0] // slices
    parts = score.shape[1] // LANES
    odd = index_ref[0] % 2 != 0
    for place, owners in enumerate(zip(*orders)):
        pieces = [owner % slices for owner in owners]
        blocks = [score[piece * rows : (piece + 1) * rows, :] for piece in pieces]
        block = blocks[0] if pieces[0] == pieces[1] else jnp.where(odd, blocks[1], blocks[0])
        for part in range(parts):
            score_ref[pl.ds((place * parts + part) * rows, rows), :] = block[:, part * LANES : (part + 1) * LANES]


def each(count, step):
    if count <= UNROLLED:
        for i in range(count):
            step(i)
    else:
        pl.loop(0, count)(step)


def gram_kernel(orders, members, shares, index_ref, moved_ref, gram_ref, centered_ref, lanes_ref):
    samples = len(orders[0])
    odd = index_ref[0] % 2 != 0
    width = samples // shares
    rows = moved_ref.shape[0] // samples
    scores = [moved_ref[pl.ds(place * rows, rows), :] for place in range(samples)]
    mean = functools.reduce(jnp.add, scores) * (1.0 / samples)
    for place, (even_owner, odd_owner) in enumerate(zip(*orders)):
        centered_ref[jnp.where(odd, odd_owner, even_owner)] = scores[place] - mean
    mine = members // shares
    first = index_ref[0] // 2 * mine

    def row_step(row):
        own = centered_ref[first + row]
        for share in range(shares):
            def column_step(column):
                product = own * centered_ref[share * width + column]
                place = members - 1 - (row * shares + share)
                lanes_ref[column, pl.ds(place, 1), :] = jnp.sum(product, axis=0, keepdims=True)

            each(width, column_step)

    each(mine, row_step)
    lane = lax.broadcasted_iota(jnp.int32, (members, LANES), 1)
    gram = jnp.zeros((members, LANES), jnp.float32)
    for column in range(width):
        gram = jnp.where(lane == column, jnp.sum(lanes_ref[column], axis=1, keepdims=True), gram)
    gram_ref[...] = gram * (1.0 / samples)


def body(spins, activations, gradients):
    n_dev, n_rep = lax.axis_size("dev"), lax.axis_size("rep")
    act, grad = activations[0, 0], gradients[0, 0]
    channels, outputs = act.shape[1], grad.shape[1]
    width = n_dev // n_rep
    layers = n_dev // 2
    orders = [
        [2 * layer + j for j in (1, 0) for layer in along]
        for along in (
            [i ^ (i >> 1) ^ (layers // 2) for i in range(layers)],
            [(layers // 2 - i) % layers for i in range(layers)],
        )
    ]
    members = n_dev * n_rep // 2
    goal = [members - 1 - place for place in range(members)]
    size = channels * outputs // LANES // (n_dev // 2)
    index = (lax.axis_index("dev") // (n_dev // 2) * 2 + lax.axis_index("rep") % 2).astype(jnp.int32).reshape(1)
    score = pl.pallas_call(
        functools.partial(score_kernel, orders),
        out_shape=jax.ShapeDtypeStruct((n_dev * size, LANES), jnp.float32),
        in_specs=[SMEM, HBM, HBM, HBM],
        out_specs=VMEM,
        scratch_shapes=[
            pltpu.VMEM(spins.shape, spins.dtype),
            pltpu.VMEM(act.shape, act.dtype),
            pltpu.VMEM(grad.shape, grad.dtype),
            pltpu.SemaphoreType.DMA((4,)),
        ],
        compiler_params=PARAMS,
        name="score",
    )(index, *(pltpu.with_memory_space_constraint(x, pltpu.HBM) for x in (spins, act, grad)))
    columns = [[d * n_rep + r for d in orders[r % 2]] for r in range(n_rep)]
    moved = lax.all_to_all(
        score, ("dev", "rep"), split_axis=0, concat_axis=0, tiled=True, axis_index_groups=columns
    )
    partial = pl.pallas_call(
        functools.partial(gram_kernel, orders, members, n_rep),
        out_shape=jax.ShapeDtypeStruct((members, LANES), jnp.float32),
        in_specs=[SMEM, VMEM],
        out_specs=VMEM,
        scratch_shapes=[
            pltpu.VMEM((n_dev, size, LANES), jnp.float32),
            pltpu.VMEM((width, members, LANES), jnp.float32),
        ],
        compiler_params=PARAMS,
        name="gram",
    )(index, moved)
    groups = [[half * members + member for member in goal] for half in range(2)]
    parts = lax.all_to_all(
        partial, ("dev", "rep"), split_axis=0, concat_axis=0, tiled=True, axis_index_groups=groups
    )
    return jnp.sum(parts, axis=0, keepdims=True)[:, :width]


def solution(mesh):
    return jax.shard_map(
        body,
        mesh=mesh,
        in_specs=(P("dev", None), P("rep", "dev", None, None), P("rep", "dev", None, None)),
        out_specs=P("dev", "rep"),
        check_vma=False,
    )
```
